32 devices in a mesh: ctxa: 4 (over z), ctxb: 8 (over y, x, core).
Axes of the slice: x: 2, y: 2, z: 4, core: 2. Of those that a mesh axis runs over, the one named last changes fastest.
Arguments:
- queries: bfloat16 [8192, 8, 128], P(('ctxa', 'ctxb')), may hold values from -14 to 14
- key_vectors: bfloat16 [8192, 128], P(('ctxa', 'ctxb')), may hold values from -5 to 5
- value_vectors: bfloat16 [8192, 128], P(('ctxa', 'ctxb')), may hold values from -12 to 12
- out_grad: bfloat16 [8192, 8, 128], P(('ctxa', 'ctxb')), may hold values from -6 to 6
Outputs:
- attention: bfloat16 [8192, 8, 128], P(('ctxa', 'ctxb'))
- query_grad: bfloat16 [8192, 8, 128], P(('ctxa', 'ctxb'))
- key_grad: bfloat16 [8192, 128], P(('ctxa', 'ctxb'))
- value_grad: bfloat16 [8192, 128], P(('ctxa', 'ctxb'))
The draws below stay inside these ranges and needn't reach their ends.
All inputs are finite; a program needn't handle non-finite values.
Results may differ from the reference program's by a relative error of at most 0.012.
Values may be sent and summed in bfloat16 or wider, within the bound.
No kernel may reach another device: no remote copies, remote signals or barrier semaphores. Data moves between devices by JAX's collectives and lax.ppermute only.
A program may use at most 64 MiB of HBM per device.

```python
import jax
import jax.numpy as jnp
from jax import lax

HQ = 8
DH = 128
BLK = 128
WIN = 1024
FAR = 6
TOKENS = 8192


def draw_queries(key, part):
    base_key = jax.random.fold_in(key, 11)
    return jnp.clip(2.0 * jax.random.normal(base_key, (TOKENS, HQ, DH), jnp.float32), -10.0, 10.0).astype(jnp.bfloat16)


def draw_key_vectors(key, part):
    base_key = jax.random.fold_in(key, 13)
    return jnp.clip(jax.random.normal(base_key, (TOKENS, DH), jnp.float32), -5.0, 5.0).astype(jnp.bfloat16)


def shard_levels(own_key, shape, cuts, low, top_value):
    def one(dim, parts):
        steps = jax.random.uniform(jax.random.fold_in(jax.random.fold_in(own_key, 6), dim), (parts,), jnp.float32, low / len(cuts), top_value / len(cuts))
        return jnp.repeat(jnp.exp(steps), shape[dim] // parts).reshape((-1,) + (1,) * (len(shape) - dim - 1))

    gain = one(*cuts[0])
    for cut in cuts[1:]:
        gain = gain * one(*cut)
    return gain


def normal_values(own_key, shape, spread, limit, pieces=(), kind=jnp.bfloat16):
    drawn = spread * jax.random.normal(own_key, shape, jnp.float32)
    if pieces:
        drawn = drawn * shard_levels(own_key, shape, pieces, -0.22, 0.18)
    return jnp.clip(drawn, -limit, limit).astype(kind)


def setup_inputs(seed: int = 0) -> dict:
    seeds = jax.random.split(jax.random.key(seed), 5)
    return {
        "queries": draw_queries(jax.random.fold_in(seeds[4], 71), 0),
        "key_vectors": draw_key_vectors(jax.random.fold_in(seeds[4], 71), 0),
        "value_vectors": normal_values(seeds[2], (TOKENS, DH), 2.0, 12.0, ((0, 32),)),
        "out_grad": normal_values(seeds[3], (TOKENS, HQ, DH), 1.0, 6.0, ((0, 32),)),
    }


def reference(queries, key_vectors, value_vectors, out_grad):
    score_scale = 1.0 / (DH ** 0.5)
    stride = 2 * WIN // BLK
    key_span = WIN + BLK
    row_count = BLK * HQ
    total_keys = key_span + FAR * BLK
    offsets = jnp.arange(key_span, dtype=jnp.int32)
    inside = jnp.arange(BLK, dtype=jnp.int32)
    block_count = TOKENS // BLK

    def one_block(running, block_index):
        block_start = (block_index * BLK).astype(jnp.int32)
        q_rows = lax.dynamic_slice_in_dim(queries, block_start, BLK, 0).reshape(row_count, DH)
        grad_rows = lax.dynamic_slice_in_dim(out_grad, block_start, BLK, 0).reshape(row_count, DH)
        near_start = jnp.maximum(block_start - WIN, 0).astype(jnp.int32)
        q_pos = block_start + inside
        k_pos = near_start + offsets
        starts = [near_start]
        lengths = [key_span]
        masks = [(k_pos[None, :] > q_pos[:, None] - WIN) & (k_pos[None, :] <= q_pos[:, None])]
        for level_index in range(FAR):
            far_block = block_index - stride * (2 ** level_index)
            starts.append((jnp.maximum(far_block, 0) * BLK).astype(jnp.int32))
            lengths.append(BLK)
            masks.append(jnp.broadcast_to(far_block >= 0, (BLK, BLK)))
        key_rows = jnp.concatenate([lax.dynamic_slice_in_dim(key_vectors, begin, size, 0) for begin, size in zip(starts, lengths)], axis=0)
        value_rows = jnp.concatenate([lax.dynamic_slice_in_dim(value_vectors, begin, size, 0) for begin, size in zip(starts, lengths)], axis=0)
        visible = jnp.concatenate(masks, axis=1)
        visible = jnp.broadcast_to(visible[:, None, :], (BLK, HQ, total_keys)).reshape(row_count, total_keys)
        scores = jnp.einsum("rd,kd->rk", q_rows.astype(jnp.float32), key_rows.astype(jnp.float32)) * score_scale
        scores = jnp.where(visible, scores, -jnp.inf)
        row_max = jnp.max(scores, axis=1, keepdims=True)
        log_total = row_max + jnp.log(jnp.sum(jnp.exp(scores - row_max), axis=1, keepdims=True))
        probs = jnp.exp(scores - log_total)
        probs_low = probs.astype(jnp.bfloat16)
        out_rows = jnp.dot(probs_low, value_rows, preferred_element_type=jnp.float32).astype(jnp.bfloat16)
        row_delta = jnp.sum(grad_rows.astype(jnp.float32) * out_rows.astype(jnp.float32), axis=1, keepdims=True)
        prob_grad = jnp.einsum("rd,kd->rk", grad_rows.astype(jnp.float32), value_rows.astype(jnp.float32))
        score_grad = (probs * (prob_grad - row_delta)).astype(jnp.bfloat16)
        q_grad_rows = (jnp.dot(score_grad, key_rows, preferred_element_type=jnp.float32) * score_scale).astype(jnp.bfloat16)
        key_terms = jnp.einsum("rk,rd->kd", score_grad.astype(jnp.float32), q_rows.astype(jnp.float32)) * score_scale
        value_terms = jnp.einsum("rk,rd->kd", probs_low.astype(jnp.float32), grad_rows.astype(jnp.float32))
        grad_terms = jnp.stack([key_terms, value_terms])
        position = 0
        for begin, size in zip(starts, lengths):
            previous = lax.dynamic_slice_in_dim(running, begin, size, 1)
            running = lax.dynamic_update_slice_in_dim(running, previous + grad_terms[:, position:position + size], begin, 1)
            position = position + size
        return running, (out_rows.reshape(BLK, HQ, DH), q_grad_rows.reshape(BLK, HQ, DH))

    running = jnp.zeros((2, TOKENS, DH), jnp.float32)
    running, outputs = lax.scan(one_block, running, jnp.arange(block_count, dtype=jnp.int32))
    attention = outputs[0].reshape(TOKENS, HQ, DH)
    query_grad = outputs[1].reshape(TOKENS, HQ, DH)
    return attention, query_grad, running[0].astype(jnp.bfloat16), running[1].astype(jnp.bfloat16)
```

```python
import functools

import jax
import jax.numpy as jnp
from jax import lax
from jax.experimental import pallas as pl
from jax.experimental.pallas import tpu as pltpu
from jax.sharding import PartitionSpec as P

BLK = 128
WIN = 1024
FAR = 6
ROWS = 256
AXES = ("ctxa", "ctxb")
NEG = -1e30
BIG = 1e30
LOG2E = 1.4426950408889634
NT = (((1,), (1,)), ((), ()))
NN = (((1,), (0,)), ((), ()))


def dot(a, b, dims):
    return lax.dot_general(a, b, dims, preferred_element_type=jnp.float32)


def attention_kernel(plan, *refs):
    tok, heads, width, near, distances = plan
    pieces = len(near) + len(distances)
    q_ref, g_ref = refs[0], refs[1]
    kv_refs = refs[2 : 2 + pieces]
    att_ref, qg_ref = refs[2 + pieces], refs[3 + pieces]
    kvg_refs = refs[4 + pieces : 4 + 2 * pieces]
    k_c, v_c, kt_c, vt_c, dk_c, dv_c, s_c, p_c, d_c, grads = refs[4 + 2 * pieces :]
    per = tok // BLK
    win_blocks = WIN // BLK + 1
    levels = len(distances)
    blocks = win_blocks + levels
    block = pl.program_id(0)
    tile = pl.program_id(1)
    tiles = pl.num_programs(1)
    device = lax.axis_index(AXES)
    scale = 1.0 / width**0.5

    def source(block_index, part):
        if part < win_blocks:
            piece, offset = divmod(block_index + part, per)
            return piece, offset * BLK
        return len(near) + part - win_blocks, block_index * BLK

    def valid(part):
        if part < win_blocks:
            return device * per + block + part >= win_blocks - 1
        return device >= distances[part - win_blocks]

    @pl.when((block == 0) & (tile == 0))
    def _():
        grads[...] = jnp.zeros_like(grads)
        lane = lax.broadcasted_iota(jnp.int32, (blocks * BLK, width), 1)
        v_c[:, width:] = jnp.where(lane < 3, 1.0, 0.0).astype(jnp.bfloat16)
        vt_c[width:, :] = jnp.ones((16, blocks * BLK), jnp.bfloat16)

    for index in range(per):

        @pl.when((block == index) & (tile == 0))
        def _():
            for part in range(blocks):
                piece, offset = source(index, part)
                rows = slice(part * BLK, (part + 1) * BLK)
                keys = kv_refs[piece][0, offset : offset + BLK, :]
                values = kv_refs[piece][1, offset : offset + BLK, :]
                k_c[rows, :width] = keys
                k_c[rows, width:] = keys
                v_c[rows, :width] = values
                kt_c[:, rows] = keys.T
                vt_c[:width, rows] = values.T

    q = q_ref[...]
    g = g_ref[...]
    scaled = q.astype(jnp.float32) * (scale * LOG2E)
    q_hi = scaled.astype(jnp.bfloat16)
    q_lo = (scaled - q_hi.astype(jnp.float32)).astype(jnp.bfloat16)
    q_aug = jnp.concatenate([q_hi, q_lo], axis=1)
    s_c[...] = dot(k_c[...], q_aug, NT)
    key_in = lax.broadcasted_iota(jnp.int32, (BLK, ROWS), 0)
    tok_in = lax.broadcasted_iota(jnp.int32, (BLK, ROWS), 1) // heads + tile * (ROWS // heads)
    newest = slice((win_blocks - 1) * BLK, win_blocks * BLK)
    s_c[:BLK, :] = jnp.where(key_in > tok_in, s_c[:BLK, :], NEG)
    s_c[newest, :] = jnp.where(key_in <= tok_in, s_c[newest, :], NEG)
    top = jnp.full((8, ROWS), NEG, jnp.float32)
    for part in range(blocks):
        rows = slice(part * BLK, (part + 1) * BLK)
        part_top = jnp.max(s_c[rows, :].reshape(BLK // 8, 8, ROWS), axis=0)
        top = jnp.maximum(top, jnp.where(valid(part), part_top, NEG))
    row_max = jnp.max(top, axis=0, keepdims=True)
    for part in range(blocks):
        rows = slice(part * BLK, (part + 1) * BLK)
        shift = jnp.where(valid(part), row_max, BIG)
        p_c[rows, :] = jnp.exp2(s_c[rows, :] - shift).astype(jnp.bfloat16)
    acc = dot(vt_c[...], p_c[...], NN)
    inverse = 1.0 / acc[width : width + 1, :]
    att = (acc[:width, :] * inverse).T.astype(jnp.bfloat16)
    att_ref[...] = att
    g_norm = (g.astype(jnp.float32) * jnp.broadcast_to(inverse, (width, ROWS)).T).astype(jnp.bfloat16)
    delta = -jnp.sum(g_norm.astype(jnp.float32) * att.astype(jnp.float32), axis=1, keepdims=True)
    d_hi = delta.astype(jnp.bfloat16).astype(jnp.float32)
    d_mid = (delta - d_hi).astype(jnp.bfloat16).astype(jnp.float32)
    d_lo = delta - d_hi - d_mid
    lane = lax.broadcasted_iota(jnp.int32, (ROWS, width), 1)
    tail = jnp.where(lane == 0, d_hi, jnp.where(lane == 1, d_mid, jnp.where(lane == 2, d_lo, 0.0)))
    g_aug = jnp.concatenate([g_norm, tail.astype(jnp.bfloat16)], axis=1)
    d_c[...] = (p_c[...].astype(jnp.float32) * dot(v_c[...], g_aug, NT)).astype(jnp.bfloat16)
    dv = dot(p_c[...], g_norm, NN)
    dk = dot(d_c[...], q, NN)

    @pl.when(tile == 0)
    def _():
        dv_c[...] = dv
        dk_c[...] = dk

    @pl.when(tile > 0)
    def _():
        dv_c[...] += dv
        dk_c[...] += dk

    dq = dot(kt_c[...], d_c[...], NN)
    qg_ref[...] = (dq * scale).T.astype(jnp.bfloat16)

    for index in range(per):

        @pl.when((block == index) & (tile == tiles - 1))
        def _():
            for part in range(blocks):
                piece, offset = source(index, part)
                rows = slice(part * BLK, (part + 1) * BLK)
                grads[piece, 0, offset : offset + BLK, :] += dk_c[rows, :] * scale
                grads[piece, 1, offset : offset + BLK, :] += dv_c[rows, :]

    @pl.when((block == per - 1) & (tile == tiles - 1))
    def _():
        for piece in range(pieces):
            kvg_refs[piece][...] = grads[piece].astype(kvg_refs[piece].dtype)


def attend(q_rows, g_rows, kv_pieces, plan):
    tok, heads, width, near, distances = plan
    pieces = len(kv_pieces)
    blocks = WIN // BLK + 1 + len(distances)
    keys = blocks * BLK
    tiles = BLK * heads // ROWS
    row_spec = pl.BlockSpec((ROWS, width), lambda b, t: (b * tiles + t, 0))
    kv_spec = pl.BlockSpec((2, tok, width), lambda b, t: (0, 0, 0))
    row_shape = jax.ShapeDtypeStruct(q_rows.shape, jnp.bfloat16)
    own = len(near) - 1
    kvg_shapes = [
        jax.ShapeDtypeStruct((2, tok, width), jnp.float32 if i == own else jnp.bfloat16)
        for i in range(pieces)
    ]
    bf16, f32 = jnp.bfloat16, jnp.float32
    return pl.pallas_call(
        functools.partial(attention_kernel, plan),
        out_shape=[row_shape, row_shape] + kvg_shapes,
        grid=(tok // BLK, tiles),
        in_specs=[row_spec, row_spec] + [kv_spec] * pieces,
        out_specs=[row_spec, row_spec] + [kv_spec] * pieces,
        scratch_shapes=[
            pltpu.VMEM((keys, 2 * width), bf16),
            pltpu.VMEM((keys, 2 * width), bf16),
            pltpu.VMEM((width, keys), bf16),
            pltpu.VMEM((width + 16, keys), bf16),
            pltpu.VMEM((keys, width), f32),
            pltpu.VMEM((keys, width), f32),
            pltpu.VMEM((keys, ROWS), f32),
            pltpu.VMEM((keys, ROWS), bf16),
            pltpu.VMEM((keys, ROWS), bf16),
            pltpu.VMEM((pieces, 2, tok, width), f32),
        ],
        compiler_params=pltpu.CompilerParams(
            dimension_semantics=("arbitrary", "arbitrary"), vmem_limit_bytes=56 << 20
        ),
    )(q_rows, g_rows, *kv_pieces)


def shifted(value, by):
    count = lax.axis_size(AXES)
    return lax.ppermute(value, AXES, [(i, (i + by) % count) for i in range(count)])


def body(queries, key_vectors, value_vectors, out_grad):
    tok, heads, width = queries.shape
    devices_all = lax.axis_size(AXES)
    device = lax.axis_index(AXES)
    shards = WIN // tok
    stride = 2 * WIN // tok
    paired = jnp.stack([key_vectors, value_vectors])
    distances = tuple(
        stride * 2**level for level in range(FAR) if stride * 2**level < devices_all
    )
    near = tuple(range(shards, -1, -1))
    offsets = near[:-1] + (0,) + distances
    kv_pieces = [paired if by == 0 else shifted(paired, by) for by in offsets]
    plan = (tok, heads, width, near, distances)
    outs = attend(
        queries.reshape(tok * heads, width), out_grad.reshape(tok * heads, width), kv_pieces, plan
    )
    attention, query_grad = outs[0], outs[1]
    own_grad = None
    total = outs[2 + shards]
    for by, terms in zip(offsets, outs[2:]):
        if by:
            total = total + shifted(terms, -by).astype(jnp.float32)
    return (
        attention.reshape(queries.shape),
        query_grad.reshape(queries.shape),
        total[0].astype(jnp.bfloat16),
        total[1].astype(jnp.bfloat16),
    )


def solution(mesh):
    rows = P(AXES, None, None)
    keys = P(AXES, None)
    return jax.shard_map(
        body,
        mesh=mesh,
        in_specs=(rows, keys, keys, rows),
        out_specs=(rows, rows, keys, keys),
        check_vma=False,
    )
```

```python
import functools

import jax
import jax.numpy as jnp
from jax import lax
from jax.experimental import pallas as pl
from jax.experimental.pallas import tpu as pltpu
from jax.sharding import PartitionSpec as P

BLK = 128
WIN = 1024
FAR = 6
ROWS = 1024
AXES = ("ctxa", "ctxb")
NEG = -1e30
BIG = 1e30
LOG2E = 1.4426950408889634
NT = (((1,), (1,)), ((), ()))
NN = (((1,), (0,)), ((), ()))


def dot(a, b, dims):
    return lax.dot_general(a, b, dims, preferred_element_type=jnp.float32)


def attention_kernel(plan, *refs):
    tok, heads, width, near, distances = plan
    pieces = len(near) + len(distances)
    q_ref, g_ref = refs[0], refs[1]
    kv_refs = refs[2 : 2 + pieces]
    att_ref, qg_ref = refs[2 + pieces], refs[3 + pieces]
    kvg_refs = refs[4 + pieces : 4 + 2 * pieces]
    k_c, v_c, kt_c, vt_c, dk_c, dv_c, s_c, p_c, d_c, grads = refs[4 + 2 * pieces :]
    per = tok // BLK
    win_blocks = WIN // BLK + 1
    levels = len(distances)
    blocks = win_blocks + levels
    block = pl.program_id(0)
    tile = pl.program_id(1)
    tiles = pl.num_programs(1)
    device = lax.axis_index(AXES)
    scale = 1.0 / width**0.5

    def source(block_index, part):
        if part < win_blocks:
            piece, offset = divmod(block_index + part, per)
            return piece, offset * BLK
        return len(near) + part - win_blocks, block_index * BLK

    def valid(part):
        if part < win_blocks:
            return device * per + block + part >= win_blocks - 1
        return device >= distances[part - win_blocks]

    @pl.when((block == 0) & (tile == 0))
    def _():
        grads[...] = jnp.zeros_like(grads)
        lane = lax.broadcasted_iota(jnp.int32, (blocks * BLK, width), 1)
        v_c[:, width:] = jnp.where(lane < 3, 1.0, 0.0).astype(jnp.bfloat16)
        vt_c[width:, :] = jnp.ones((16, blocks * BLK), jnp.bfloat16)

    for index in range(per):

        @pl.when((block == index) & (tile == 0))
        def _():
            for part in range(blocks):
                piece, offset = source(index, part)
                rows = slice(part * BLK, (part + 1) * BLK)
                keys = kv_refs[piece][0, offset : offset + BLK, :]
                values = kv_refs[piece][1, offset : offset + BLK, :]
                k_c[rows, :width] = keys
                k_c[rows, width:] = keys
                v_c[rows, :width] = values
                kt_c[:, rows] = keys.T
                vt_c[:width, rows] = values.T

    q = q_ref[...]
    g = g_ref[...]
    scaled = q.astype(jnp.float32) * (scale * LOG2E)
    q_hi = scaled.astype(jnp.bfloat16)
    q_lo = (scaled - q_hi.astype(jnp.float32)).astype(jnp.bfloat16)
    q_aug = jnp.concatenate([q_hi, q_lo], axis=1)
    s_c[...] = dot(k_c[...], q_aug, NT)
    key_in = lax.broadcasted_iota(jnp.int32, (BLK, ROWS), 0)
    tok_in = lax.broadcasted_iota(jnp.int32, (BLK, ROWS), 1) // heads + tile * (ROWS // heads)
    newest = slice((win_blocks - 1) * BLK, win_blocks * BLK)
    s_c[:BLK, :] = jnp.where(key_in > tok_in, s_c[:BLK, :], NEG)
    s_c[newest, :] = jnp.where(key_in <= tok_in, s_c[newest, :], NEG)
    top = jnp.full((8, ROWS), NEG, jnp.float32)
    for part in range(blocks):
        rows = slice(part * BLK, (part + 1) * BLK)
        part_top = jnp.max(s_c[rows, :].reshape(BLK // 8, 8, ROWS), axis=0)
        top = jnp.maximum(top, jnp.where(valid(part), part_top, NEG))
    row_max = jnp.max(top, axis=0, keepdims=True)
    for part in range(blocks):
        rows = slice(part * BLK, (part + 1) * BLK)
        shift = jnp.where(valid(part), row_max, BIG)
        p_c[rows, :] = jnp.exp2(s_c[rows, :] - shift).astype(jnp.bfloat16)
    acc = dot(vt_c[...], p_c[...], NN)
    inverse = 1.0 / acc[width : width + 1, :]
    att = (acc[:width, :] * inverse).T.astype(jnp.bfloat16)
    att_ref[...] = att
    g_norm = (g.astype(jnp.float32) * jnp.broadcast_to(inverse, (width, ROWS)).T).astype(jnp.bfloat16)
    delta = -jnp.sum(g_norm.astype(jnp.float32) * att.astype(jnp.float32), axis=1, keepdims=True)
    d_hi = delta.astype(jnp.bfloat16).astype(jnp.float32)
    d_mid = (delta - d_hi).astype(jnp.bfloat16).astype(jnp.float32)
    d_lo = delta - d_hi - d_mid
    lane = lax.broadcasted_iota(jnp.int32, (ROWS, width), 1)
    tail = jnp.where(lane == 0, d_hi, jnp.where(lane == 1, d_mid, jnp.where(lane == 2, d_lo, 0.0)))
    g_aug = jnp.concatenate([g_norm, tail.astype(jnp.bfloat16)], axis=1)
    d_c[...] = (p_c[...].astype(jnp.float32) * dot(v_c[...], g_aug, NT)).astype(jnp.bfloat16)
    dv = dot(p_c[...], g_norm, NN)
    dk = dot(d_c[...], q, NN)

    @pl.when(tile == 0)
    def _():
        dv_c[...] = dv
        dk_c[...] = dk

    @pl.when(tile > 0)
    def _():
        dv_c[...] += dv
        dk_c[...] += dk

    dq = dot(kt_c[...], d_c[...], NN)
    qg_ref[...] = (dq * scale).T.astype(jnp.bfloat16)

    for index in range(per):

        @pl.when((block == index) & (tile == tiles - 1))
        def _():
            for part in range(blocks):
                piece, offset = source(index, part)
                rows = slice(part * BLK, (part + 1) * BLK)
                grads[piece, 0, offset : offset + BLK, :] += dk_c[rows, :] * scale
                grads[piece, 1, offset : offset + BLK, :] += dv_c[rows, :]

    @pl.when((block == per - 1) & (tile == tiles - 1))
    def _():
        for piece in range(pieces):
            kvg_refs[piece][...] = grads[piece].astype(kvg_refs[piece].dtype)


def attend(q_rows, g_rows, kv_pieces, plan):
    tok, heads, width, near, distances = plan
    pieces = len(kv_pieces)
    blocks = WIN // BLK + 1 + len(distances)
    keys = blocks * BLK
    tiles = BLK * heads // ROWS
    row_spec = pl.BlockSpec((ROWS, width), lambda b, t: (b * tiles + t, 0))
    kv_spec = pl.BlockSpec((2, tok, width), lambda b, t: (0, 0, 0))
    row_shape = jax.ShapeDtypeStruct(q_rows.shape, jnp.bfloat16)
    own = len(near) - 1
    kvg_shapes = [
        jax.ShapeDtypeStruct((2, tok, width), jnp.float32 if i == own else jnp.bfloat16)
        for i in range(pieces)
    ]
    bf16, f32 = jnp.bfloat16, jnp.float32
    return pl.pallas_call(
        functools.partial(attention_kernel, plan),
        out_shape=[row_shape, row_shape] + kvg_shapes,
        grid=(tok // BLK, tiles),
        in_specs=[row_spec, row_spec] + [kv_spec] * pieces,
        out_specs=[row_spec, row_spec] + [kv_spec] * pieces,
        scratch_shapes=[
            pltpu.VMEM((keys, 2 * width), bf16),
            pltpu.VMEM((keys, 2 * width), bf16),
            pltpu.VMEM((width, keys), bf16),
            pltpu.VMEM((width + 16, keys), bf16),
            pltpu.VMEM((keys, width), f32),
            pltpu.VMEM((keys, width), f32),
            pltpu.VMEM((keys, ROWS), f32),
            pltpu.VMEM((keys, ROWS), bf16),
            pltpu.VMEM((keys, ROWS), bf16),
            pltpu.VMEM((pieces, 2, tok, width), f32),
        ],
        compiler_params=pltpu.CompilerParams(
            dimension_semantics=("arbitrary", "arbitrary"), vmem_limit_bytes=56 << 20
        ),
    )(q_rows, g_rows, *kv_pieces)


def shifted(value, by):
    count = lax.axis_size(AXES)
    return lax.ppermute(value, AXES, [(i, (i + by) % count) for i in range(count)])


def body(queries, key_vectors, value_vectors, out_grad):
    tok, heads, width = queries.shape
    devices_all = lax.axis_size(AXES)
    device = lax.axis_index(AXES)
    shards = WIN // tok
    stride = 2 * WIN // tok
    paired = jnp.stack([key_vectors, value_vectors])
    distances = tuple(
        stride * 2**level for level in range(FAR) if stride * 2**level < devices_all
    )
    near = tuple(range(shards, -1, -1))
    offsets = near[:-1] + (0,) + distances
    kv_pieces = [paired if by == 0 else shifted(paired, by) for by in offsets]
    plan = (tok, heads, width, near, distances)
    outs = attend(
        queries.reshape(tok * heads, width), out_grad.reshape(tok * heads, width), kv_pieces, plan
    )
    attention, query_grad = outs[0], outs[1]
    own_grad = None
    total = outs[2 + shards]
    for by, terms in zip(offsets, outs[2:]):
        if by:
            total = total + shifted(terms, -by).astype(jnp.float32)
    return (
        attention.reshape(queries.shape),
        query_grad.reshape(queries.shape),
        total[0].astype(jnp.bfloat16),
        total[1].astype(jnp.bfloat16),
    )


def solution(mesh):
    rows = P(AXES, None, None)
    keys = P(AXES, None)
    return jax.shard_map(
        body,
        mesh=mesh,
        in_specs=(rows, keys, keys, rows),
        out_specs=(rows, rows, keys, keys),
        check_vma=False,
    )
```

```python
import functools

import jax
import jax.numpy as jnp
from jax import lax
from jax.experimental import pallas as pl
from jax.experimental.pallas import tpu as pltpu
from jax.sharding import PartitionSpec as P

BLK = 128
WIN = 1024
FAR = 6
AXES = ("ctxa", "ctxb")
NEG = -1e30
BIG = 1e30
LOG2E = 1.4426950408889634
NT = (((1,), (1,)), ((), ()))
NN = (((1,), (0,)), ((), ()))
RELAY_IN = True
RELAY_OUT = False
BF16, F32 = jnp.bfloat16, jnp.float32


def dot(a, b, dims):
    return lax.dot_general(a, b, dims, preferred_element_type=F32)


class Plan:
    def __init__(self, tok, heads, width, shards, distances):
        self.tok, self.heads, self.width = tok, heads, width
        self.shards, self.distances = shards, distances
        self.per = tok // BLK
        self.rows = BLK * heads
        self.scale = 1.0 / width**0.5
        self.win = WIN // BLK + 1
        self.blocks = self.win + len(distances)
        self.keys = self.blocks * BLK
        self.parts = [self.order(block) for block in range(self.per)]

    def order(self, block):
        groups = {"far": [], "odd": [], "own": [], "even": []}
        for level in range(len(self.distances)):
            groups["far"].append((level, block * BLK, None))
        for part in range(self.win):
            piece, offset = divmod(block + part, self.per)
            behind = self.shards - piece
            if behind == 0:
                groups["own"].append((0, offset * BLK, part))
            elif behind % 2:
                groups["odd"].append((behind // 2, offset * BLK, part))
            else:
                groups["even"].append((behind // 2 - 1, offset * BLK, part))
        return groups

    def flat(self, block):
        return [
            (name,) + entry for name in ("far", "odd", "own", "even") for entry in self.parts[block][name]
        ]

    def span(self, block, name):
        start = 0
        for group in ("far", "odd", "own", "even"):
            size = len(self.parts[block][group]) * BLK
            if group == name:
                return slice(start, start + size)
            start += size


def backward(plan, block, name, refs, grads, dq_ref, start):
    q_ref, g_ref, p_ref, v_ref, kt_ref = refs
    span = plan.span(block, name)
    rows = slice(block * plan.rows, (block + 1) * plan.rows)
    probs = p_ref[block, span, :]
    g_aug = g_ref[rows, :]
    d = (probs.astype(F32) * dot(v_ref[block, span, :], g_aug, NT)).astype(BF16)
    dv = dot(probs, g_aug[:, : plan.width], NN)
    dk = dot(d, q_ref[rows, :], NN) * plan.scale
    dq = dot(kt_ref[block, :, span], d, NN)
    if start:
        dq_ref[block] = dq
    else:
        dq_ref[block] = dq_ref[block] + dq
    for index, (slot, offset, _) in enumerate(plan.parts[block][name]):
        part = slice(index * BLK, (index + 1) * BLK)
        keys = slice(offset, offset + BLK)
        grads[slot, 0, keys, :] += dk[part]
        grads[slot, 1, keys, :] += dv[part]


def forward_kernel(plan, *refs):
    evens, levels = plan.shards // 2, len(plan.distances)
    q_ref, g_ref = refs[:2]
    near_refs = refs[2 : 3 + evens]
    swap_refs = refs[3 + evens : 4 + 2 * evens]
    far_refs = refs[4 + 2 * evens : 4 + 2 * evens + levels]
    rest = refs[4 + 2 * evens + levels :]
    att_ref, p_ref, v_ref, kt_ref, ga_ref, dq_ref = rest[:6]
    farg_refs = rest[6 : 6 + levels]
    odd_c, k_c, vt_c, s_c, grads = rest[6 + levels :]
    width, rows_n, keys_n = plan.width, plan.rows, plan.keys
    device = lax.axis_index(AXES)
    parity = device % 2

    def valid(block, name, slot, part):
        if part is None:
            return device >= plan.distances[slot]
        return device * plan.per + block + part >= plan.win - 1

    for side in range(2):

        @pl.when(parity == side)
        def _():
            for slot in range(evens):
                odd_c[slot] = swap_refs[slot + 1 - side][...]

    lane = lax.broadcasted_iota(jnp.int32, (keys_n, width), 1)
    ones = jnp.where(lane < 3, 1.0, 0.0).astype(BF16)
    key_in = lax.broadcasted_iota(jnp.int32, (BLK, rows_n), 0)
    tok_in = lax.broadcasted_iota(jnp.int32, (BLK, rows_n), 1) // plan.heads
    grads[...] = jnp.zeros_like(grads)
    for block in range(plan.per):
        rows = slice(block * rows_n, (block + 1) * rows_n)
        parts = plan.flat(block)
        v_ref[block, :, width:] = ones
        vt_c[block, width:, :] = jnp.ones((16, keys_n), BF16)
        for index, (name, slot, offset, part) in enumerate(parts):
            held = slice(index * BLK, (index + 1) * BLK)
            if name == "far":
                source = far_refs[slot]
            elif name == "odd":
                source = odd_c.at[slot]
            elif name == "own":
                source = near_refs[0]
            else:
                source = near_refs[slot + 1]
            keys = source[0, offset : offset + BLK, :]
            values = source[1, offset : offset + BLK, :]
            k_c[block, held, :width] = keys
            k_c[block, held, width:] = keys
            v_ref[block, held, :width] = values
            kt_ref[block, :, held] = keys.T
            vt_c[block, :width, held] = values.T
        scaled = q_ref[rows, :].astype(F32) * (plan.scale * LOG2E)
        q_hi = scaled.astype(BF16)
        q_lo = (scaled - q_hi.astype(F32)).astype(BF16)
        s_c[block] = dot(k_c[block], jnp.concatenate([q_hi, q_lo], axis=1), NT)
        top = jnp.full((8, rows_n), NEG, F32)
        for index, (name, slot, offset, part) in enumerate(parts):
            held = slice(index * BLK, (index + 1) * BLK)
            if part == 0:
                s_c[block, held, :] = jnp.where(key_in > tok_in, s_c[block, held, :], NEG)
            if part == plan.win - 1:
                s_c[block, held, :] = jnp.where(key_in <= tok_in, s_c[block, held, :], NEG)
            part_top = jnp.max(s_c[block, held, :].reshape(BLK // 8, 8, rows_n), axis=0)
            top = jnp.maximum(top, jnp.where(valid(block, name, slot, part), part_top, NEG))
        row_max = jnp.max(top, axis=0, keepdims=True)
        for index, (name, slot, offset, part) in enumerate(parts):
            held = slice(index * BLK, (index + 1) * BLK)
            shift = jnp.where(valid(block, name, slot, part), row_max, BIG)
            p_ref[block, held, :] = jnp.exp2(s_c[block, held, :] - shift).astype(BF16)
        acc = dot(vt_c[block], p_ref[block], NN)
        inverse = 1.0 / acc[width : width + 1, :]
        att = (acc[:width, :] * inverse).T.astype(BF16)
        att_ref[rows, :] = att
        spread = jnp.broadcast_to(inverse, (width, rows_n)).T
        g_norm = (g_ref[rows, :].astype(F32) * spread).astype(BF16)
        delta = -jnp.sum(g_norm.astype(F32) * att.astype(F32), axis=1, keepdims=True)
        d_hi = delta.astype(BF16).astype(F32)
        d_mid = (delta - d_hi).astype(BF16).astype(F32)
        d_lo = delta - d_hi - d_mid
        at = lax.broadcasted_iota(jnp.int32, (rows_n, width), 1)
        tail = jnp.where(at == 0, d_hi, jnp.where(at == 1, d_mid, jnp.where(at == 2, d_lo, 0.0)))
        ga_ref[rows, :width] = g_norm
        ga_ref[rows, width:] = tail.astype(BF16)
        backward(plan, block, "far", (q_ref, ga_ref, p_ref, v_ref, kt_ref), grads, dq_ref, True)
    for level in range(levels):
        farg_refs[level][...] = grads[level].astype(BF16)


def odd_kernel(plan, q_ref, ga_ref, p_ref, v_ref, kt_ref, dqi_ref, out_ref, dq_ref, grads):
    grads[...] = jnp.zeros_like(grads)
    dq_ref[...] = dqi_ref[...]
    for block in range(plan.per):
        backward(plan, block, "odd", (q_ref, ga_ref, p_ref, v_ref, kt_ref), grads, dq_ref, False)
    out_ref[...] = grads[...].astype(BF16)


def own_kernel(plan, q_ref, ga_ref, p_ref, v_ref, kt_ref, dqi_ref, out_ref, dq_ref):
    out_ref[...] = jnp.zeros_like(out_ref)
    dq_ref[...] = dqi_ref[...]
    for block in range(plan.per):
        backward(plan, block, "own", (q_ref, ga_ref, p_ref, v_ref, kt_ref), out_ref, dq_ref, False)


def even_kernel(plan, *refs):
    q_ref, ga_ref, p_ref, v_ref, kt_ref, dqi_ref, recv_ref = refs[:7]
    evens = plan.shards // 2
    out_refs, qg_ref = refs[7 : 7 + evens], refs[7 + evens]
    grads, dq_c = refs[8 + evens :]
    parity = lax.axis_index(AXES) % 2
    dq_c[...] = dqi_ref[...]

    @pl.when(parity == 0)
    def _():
        for slot in range(evens):
            if slot + 1 < evens:
                grads[slot] = recv_ref[slot + 1].astype(F32)
            else:
                grads[slot] = jnp.zeros_like(grads[slot])

    @pl.when(parity == 1)
    def _():
        for slot in range(evens):
            grads[slot] = recv_ref[slot].astype(F32)

    for block in range(plan.per):
        backward(plan, block, "even", (q_ref, ga_ref, p_ref, v_ref, kt_ref), grads, dq_c, False)
        rows = slice(block * plan.rows, (block + 1) * plan.rows)
        qg_ref[rows, :] = (dq_c[block] * plan.scale).T.astype(BF16)
    for slot in range(evens):
        out_refs[slot][...] = grads[slot].astype(BF16)


def sum_kernel(count, *refs):
    own_ref, recv_ref = refs[:2]
    term_refs = refs[2 : 2 + count]
    kg_ref, vg_ref = refs[2 + count :]
    keep = (lax.axis_index(AXES) % 2 == 0).astype(F32)
    for index, out_ref in enumerate((kg_ref, vg_ref)):
        total = own_ref[0, index] + recv_ref[0, index].astype(F32) * keep
        for term in term_refs:
            total = total + term[index].astype(F32)
        out_ref[...] = total.astype(BF16)


def call(kernel, outs, args, scratch=(), limit=40, name=None):
    vmem = pl.BlockSpec(memory_space=pltpu.VMEM)
    return pl.pallas_call(
        kernel,
        out_shape=[jax.ShapeDtypeStruct(s, d) if not keep else pltpu.VMEM(s, d) for s, d, keep in outs],
        in_specs=[vmem] * len(args),
        out_specs=[vmem] * len(outs),
        scratch_shapes=list(scratch),
        compiler_params=pltpu.CompilerParams(vmem_limit_bytes=limit << 20),
        name=name,
    )(*args)


def shifted(value, by):
    count = lax.axis_size(AXES)
    return lax.ppermute(value, AXES, [(i, (i + by) % count) for i in range(count)])


def swapped(value):
    return lax.ppermute(value, AXES, [(i, i ^ 1) for i in range(lax.axis_size(AXES))])


def body(queries, key_vectors, value_vectors, out_grad):
    tok, heads, width = queries.shape
    devices_all = lax.axis_size(AXES)
    shards = WIN // tok
    stride = 2 * WIN // tok
    distances = tuple(
        stride * 2**level for level in range(FAR) if stride * 2**level < devices_all
    )
    plan = Plan(tok, heads, width, shards, distances)
    evens, per, keys = shards // 2, plan.per, plan.keys
    paired = jnp.stack([key_vectors, value_vectors])
    near = [paired] + [shifted(paired, 2 * slot + 2) for slot in range(evens)]
    swaps = [swapped(piece) for piece in near]
    far = [shifted(paired, distances[0])]
    for level in range(1, len(distances)):
        if RELAY_IN:
            far.append(shifted(far[-1], distances[level - 1]))
        else:
            far.append(shifted(paired, distances[level]))
    q_rows = queries.reshape(tok * heads, width)
    g_rows = out_grad.reshape(tok * heads, width)
    total_rows = tok * heads
    pair = (2, tok, width)
    outs = call(
        functools.partial(forward_kernel, plan),
        [
            ((total_rows, width), BF16, False),
            ((per, keys, plan.rows), BF16, True),
            ((per, keys, 2 * width), BF16, True),
            ((per, width, keys), BF16, True),
            ((total_rows, 2 * width), BF16, True),
            ((per, width, plan.rows), F32, True),
        ]
        + [(pair, BF16, False)] * len(distances),
        [q_rows, g_rows, *near, *swaps, *far],
        [
            pltpu.VMEM((evens,) + pair, BF16),
            pltpu.VMEM((per, keys, 2 * width), BF16),
            pltpu.VMEM((per, width + 16, keys), BF16),
            pltpu.VMEM((per, keys, plan.rows), F32),
            pltpu.VMEM((len(distances),) + pair, F32),
        ],
        name="forward",
    )
    attention, probs, values, keys_t, g_aug, dq = outs[:6]
    far_terms = list(outs[6:])
    shared = (q_rows, g_aug, probs, values, keys_t)
    dq_shape = ((per, width, plan.rows), F32, True)
    odd_terms, dq = call(
        functools.partial(odd_kernel, plan),
        [((evens,) + pair, BF16, False), dq_shape],
        [*shared, dq],
        [pltpu.VMEM((evens,) + pair, F32)],
        name="odd",
    )
    recv = swapped(odd_terms)
    if RELAY_OUT:
        for level in range(len(distances) - 1, 0, -1):
            far_terms[level - 1] = far_terms[level - 1] + shifted(far_terms[level], -distances[level - 1])
        returned = [shifted(far_terms[0], -distances[0])]
    else:
        returned = [shifted(term, -by) for term, by in zip(far_terms, distances)]
    own_terms, dq = call(
        functools.partial(own_kernel, plan),
        [((1,) + pair, F32, True), dq_shape],
        [*shared, dq],
        name="own",
    )
    outs = call(
        functools.partial(even_kernel, plan),
        [(pair, BF16, False)] * evens + [((total_rows, width), BF16, False)],
        [*shared, dq, recv],
        [pltpu.VMEM((evens,) + pair, F32), pltpu.VMEM((per, width, plan.rows), F32)],
        name="even",
    )
    returned += [shifted(term, -(2 * slot + 2)) for slot, term in enumerate(outs[:evens])]
    key_grad, value_grad = call(
        functools.partial(sum_kernel, len(returned)),
        [((tok, width), BF16, False)] * 2,
        [own_terms, recv, *returned],
        name="total",
    )
    return (
        attention.reshape(queries.shape),
        outs[evens].reshape(queries.shape),
        key_grad,
        value_grad,
    )


def solution(mesh):
    rows = P(AXES, None, None)
    keys = P(AXES, None)
    return jax.shard_map(
        body,
        mesh=mesh,
        in_specs=(rows, keys, keys, rows),
        out_specs=(rows, rows, keys, keys),
        check_vma=False,
    )
```
